32 devices in a mesh: row: 8 (over z, y), col: 4 (over x, core).
Axes of the slice: x: 2, y: 2, z: 4, core: 2. Of those that a mesh axis runs over, the one named last changes fastest.
Arguments:
- error: float32 [14336, 16384], P('row', 'col'), may hold values from -0.046875 to 0.046875
- covar: float32 [16384, 16384], P('row', 'col'), may hold values from -1 to 6, as said below
- basis: float32 [14336, 128], P('row'), may hold values from -6 to 6
Outputs:
- new_basis: float32 [14336, 128], P('row')
- factor: float32 [128, 128], replicated
The draws below stay inside these ranges and needn't reach their ends.
Inputs may be any that keep to these rules, and one draw needn't show every extreme that they name: covar is symmetric and positive definite.
All inputs are finite; a program needn't handle non-finite values.
Results may differ from the reference program's by a relative error of at most 0.0001.
Values sent between devices are 32-bit elements; how exact they have to be, the bound alone decides.
A program may use at most 128 MiB of HBM per device.

```python
import jax
import jax.numpy as jnp
from jax import lax

K = 16384
RANK = 128
ITERS = 2
M = 14336


def draw_covar(key, part):
    first = jax.random.fold_in(key, 11)
    second = jax.random.fold_in(key, 12)
    noise = jax.random.normal(first, (K, K), jnp.float32)
    noise = jnp.clip(noise, -4.0, 4.0)
    diagonal = jax.random.uniform(second, (K,), jnp.float32, 2.0, 5.5)
    symmetric = (noise + noise.T) * (0.35 / K ** 0.5)
    return symmetric + jnp.diag(diagonal)


def block_scale(stream_key, dims, pieces, low, high):
    gain = 1.0
    for position, blocks in pieces:
        draws = jax.random.uniform(jax.random.fold_in(jax.random.fold_in(stream_key, 6), position), (blocks,), jnp.float32, low / len(pieces), high / len(pieces))
        gain = gain * jnp.repeat(jnp.exp(draws), dims[position] // blocks).reshape((-1,) + (1,) * (len(dims) - 1 - position))
    return gain


def centred(key, dims, spread, most, cuts=(), held_as=jnp.bfloat16):
    level = block_scale(key, dims, cuts, -0.22, 0.18) if cuts else 1.0
    values = jax.random.normal(key, dims, jnp.float32) * spread * level
    return jnp.minimum(jnp.maximum(values, -most), most).astype(held_as)


def setup_inputs(seed: int = 0) -> dict:
    streams_of = jax.random.split(jax.random.key(seed), 4)
    error = centred(streams_of[0], (M, K), K ** -0.5, 0.046875, ((0, 8), (1, 4)), jnp.float32)
    covar = draw_covar(jax.random.fold_in(streams_of[3], 71), 0)
    basis = centred(streams_of[2], (M, RANK), 1.0, 6.0, ((0, 8),), jnp.float32)
    return {"error": error, "covar": covar, "basis": basis}


def reference(error, covar, basis):
    high = lax.Precision.HIGHEST
    rows_all = error.shape[0]
    current = basis
    lower = jnp.zeros((RANK, RANK), jnp.float32)
    for step in range(ITERS):
        projected = lax.dot_general(error.astype(jnp.float32), current.astype(jnp.float32), (((0,), (0,)), ((), ())), precision=high, preferred_element_type=jnp.float32)
        image = jnp.dot(covar.astype(jnp.float32), projected.astype(jnp.float32), precision=high, preferred_element_type=jnp.float32)
        block = jnp.dot(error.astype(jnp.float32), image.astype(jnp.float32), precision=high, preferred_element_type=jnp.float32)
        gram = jnp.dot(block.T.astype(jnp.float32), block.astype(jnp.float32), precision=high, preferred_element_type=jnp.float32) / rows_all
        lower = jnp.linalg.cholesky(gram)
        current = lax.linalg.triangular_solve(lower, block, left_side=False, lower=True, transpose_a=True)
    return (current, lower.T)
```

```python
import functools

import jax
import jax.numpy as jnp
from jax import lax
from jax.experimental import pallas as pl
from jax.experimental.pallas import tpu as pltpu
from jax.sharding import PartitionSpec as P

ITERS = 2
MESH = pl.DeviceIdType.MESH


def powers(n):
    return [1 << k for k in range(n.bit_length() - 1)]


def row_orders(n):
    bits = powers(n)
    return (bits, [bits[1], bits[0]] + bits[2:])


def bit_of(index, weight):
    return (index // weight) % 2


def partner(index, weight):
    return index + weight * (1 - 2 * bit_of(index, weight))


def rank_of(index, order):
    total, span = 0, 1 << len(order)
    for weight in order:
        span //= 2
        total = total + bit_of(index, weight) * span
    return total


def index_of(rank, order):
    total, span = 0, 1 << len(order)
    for weight in order:
        span //= 2
        total = total + ((rank // span) % 2) * weight
    return total


def rows_at(start, size):
    return pl.ds(pl.multiple_of(start, 8), size)


def device(axis, index):
    if axis == "row":
        return (index, lax.axis_index("col"))
    return (lax.axis_index("row"), index)


def greet(axes):
    barrier = pltpu.get_barrier_semaphore()
    count = 0
    for axis in axes:
        me = lax.axis_index(axis)
        for weight in powers(lax.axis_size(axis)):
            pl.semaphore_signal(barrier, inc=1, device_id=device(axis, partner(me, weight)), device_id_type=MESH)
            count += 1
    return barrier, count


def scatter_sum(axis, order, src, acc, landing, base, length, send, recv, slot):
    me = lax.axis_index(axis)
    start, place = base, base
    for weight in order:
        length //= 2
        side = bit_of(me, weight)
        keep, give = start + side * length, start + (1 - side) * length
        copy = pltpu.make_async_remote_copy(
            src.at[rows_at(give, length)], landing.at[pl.ds(place, length)],
            send.at[slot], recv.at[slot],
            device_id=device(axis, partner(me, weight)), device_id_type=MESH)
        copy.start()
        yield
        copy.wait()
        kept = rows_at(keep, length)
        acc[kept, :] = src[kept, :] + landing[pl.ds(place, length), :]
        src, start, place, slot = acc, keep, place + length, slot + 1


def gather(axis, order, out, base, length, send, recv, slot):
    me = lax.axis_index(axis)
    length //= 1 << len(order)
    start = base + rank_of(me, order) * length
    for weight in order[::-1]:
        copy = pltpu.make_async_remote_copy(
            out.at[rows_at(start, length)], out.at[rows_at(start, length)],
            send.at[slot], recv.at[slot],
            device_id=device(axis, partner(me, weight)), device_id_type=MESH)
        copy.start()
        yield
        copy.wait()
        start = start - bit_of(me, weight) * length
        length *= 2
        slot += 1


def run(streams):
    streams = list(streams)
    while streams:
        streams = [s for s in streams if next(s, streams) is None]


def sum_rows_kernel(x, out, acc, landing, send, recv):
    n = lax.axis_size("row")
    barrier, count = greet(["row"])
    pl.semaphore_wait(barrier, count)
    half = x.shape[0] // 2
    steps = len(powers(n))

    def stream(which, order):
        base, slot = which * half, which * 2 * steps
        yield from scatter_sum("row", order, x, acc, landing, base, half, send, recv, slot)
        size = half // n
        mine = rows_at(base + rank_of(lax.axis_index("row"), order) * size, size)
        out[mine, :] = acc[mine, :]
        yield from gather("row", order, out, base, half, send, recv, slot + steps)

    run(stream(k, order) for k, order in enumerate(row_orders(n)))


def sum_rows(x):
    slots = 4 * len(powers(lax.axis_size("row")))
    return pl.pallas_call(
        sum_rows_kernel,
        out_shape=jax.ShapeDtypeStruct(x.shape, x.dtype),
        in_specs=[pl.BlockSpec(memory_space=pltpu.VMEM)],
        out_specs=pl.BlockSpec(memory_space=pltpu.VMEM),
        scratch_shapes=[
            pltpu.VMEM(x.shape, x.dtype),
            pltpu.VMEM(x.shape, x.dtype),
            pltpu.SemaphoreType.DMA((slots,)),
            pltpu.SemaphoreType.DMA((slots,)),
        ],
        compiler_params=pltpu.CompilerParams(collective_id=1, has_side_effects=True),
    )(x)


def turn_kernel(x, out, acc, landing, send, recv):
    n, m = lax.axis_size("row"), lax.axis_size("col")
    r, c = lax.axis_index("row"), lax.axis_index("col")
    ratio = n // m
    size = x.shape[0]
    sub = size // n
    order_col = powers(m)
    orders = [row_orders(n)[k % 2] for k in range(ratio)]

    barrier, count = greet(["row", "col"])
    sources = []
    for q in range(ratio):
        t = rank_of(r, orders[q])
        sources.append((c * ratio + q, index_of(t // ratio, order_col), t))
    dests = []
    q_mine = r % ratio
    for j in range(ratio):
        t = rank_of(c, order_col) * ratio + j
        to = 0
        for q in range(ratio):
            to = to + index_of(t, orders[q]) * (1 - jnp.minimum(jnp.abs(q_mine - q), 1))
        dests.append((to, r // ratio, t))
    for a, b, _ in sources:
        @pl.when((a != r) | (b != c))
        def _():
            pl.semaphore_signal(barrier, inc=1, device_id=(a, b), device_id_type=MESH)
    for a, b, _ in dests:
        count = count + jnp.minimum(jnp.abs(a - r) + jnp.abs(b - c), 1)
    pl.semaphore_wait(barrier, count)

    run([scatter_sum("col", order_col, x, acc, landing, 0, size, send, recv, 0)])
    slot = len(order_col)

    def shift(j, a, b, t):
        return pltpu.make_async_remote_copy(
            acc.at[rows_at(t * sub, sub)], out.at[rows_at(q_mine * size + t * sub, sub)],
            send.at[slot + j], recv.at[slot + q_mine],
            device_id=(a, b), device_id_type=MESH)

    for j, (a, b, t) in enumerate(dests):
        @pl.when((a != r) | (b != c))
        def _():
            shift(j, a, b, t).start()

        @pl.when((a == r) & (b == c))
        def _():
            out[rows_at(q_mine * size + t * sub, sub), :] = acc[rows_at(t * sub, sub), :]

    def stream(q):
        a, b, t = sources[q]

        @pl.when((a != r) | (b != c))
        def _():
            pltpu.make_async_remote_copy(
                acc.at[rows_at(t * sub, sub)], out.at[rows_at(q * size + t * sub, sub)],
                send.at[slot + q], recv.at[slot + q],
                device_id=(a, b), device_id_type=MESH).wait_recv()
        yield from gather("row", orders[q], out, q * size, size, send, recv, slot + ratio + q * len(orders[q]))

    run(stream(q) for q in range(ratio))
    for j, (a, b, t) in enumerate(dests):
        @pl.when((a != r) | (b != c))
        def _():
            shift(j, a, b, t).wait_send()


def turn(x):
    n, m = lax.axis_size("row"), lax.axis_size("col")
    ratio = n // m
    slots = len(powers(m)) + ratio + ratio * len(powers(n))
    return pl.pallas_call(
        turn_kernel,
        out_shape=jax.ShapeDtypeStruct((x.shape[0] * ratio, x.shape[1]), x.dtype),
        in_specs=[pl.BlockSpec(memory_space=pltpu.VMEM)],
        out_specs=pl.BlockSpec(memory_space=pltpu.VMEM),
        scratch_shapes=[
            pltpu.VMEM(x.shape, x.dtype),
            pltpu.VMEM(x.shape, x.dtype),
            pltpu.SemaphoreType.DMA((slots,)),
            pltpu.SemaphoreType.DMA((slots,)),
        ],
        compiler_params=pltpu.CompilerParams(collective_id=2, has_side_effects=True),
    )(x)


def block_gram_kernel(x, out, gram, acc, landing, held, arrived, send, recv):
    n, m = lax.axis_size("row"), lax.axis_size("col")
    r, c = lax.axis_index("row"), lax.axis_index("col")
    order = powers(m)
    barrier, count = greet(["row", "col"])
    pl.semaphore_wait(barrier, count)
    run([scatter_sum("col", order, x, acc, landing, 0, x.shape[0], send, recv, 0)])
    size = x.shape[0] // m
    mine = rows_at(rank_of(c, order) * size, size)
    out[mine, :] = acc[mine, :]
    run([gather("col", order, out, 0, x.shape[0], send, recv, len(order))])
    block = out[...]
    held[0] = lax.dot_general(
        block, block, (((0,), (0,)), ((), ())),
        precision=lax.Precision.HIGHEST, preferred_element_type=jnp.float32)
    for step, weight in enumerate(powers(n)):
        slot = 2 * len(order) + step
        copy = pltpu.make_async_remote_copy(
            held.at[step], arrived.at[step], send.at[slot], recv.at[slot],
            device_id=device("row", partner(r, weight)), device_id_type=MESH)
        copy.start()
        copy.wait()
        held[step + 1] = held[step] + arrived[step]
    gram[...] = held[len(powers(n))] / (x.shape[0] * n)


def block_gram(x):
    n, m = lax.axis_size("row"), lax.axis_size("col")
    steps = len(powers(n))
    slots = 2 * len(powers(m)) + steps
    width = x.shape[1]
    return pl.pallas_call(
        block_gram_kernel,
        out_shape=(jax.ShapeDtypeStruct(x.shape, x.dtype), jax.ShapeDtypeStruct((width, width), x.dtype)),
        in_specs=[pl.BlockSpec(memory_space=pltpu.VMEM)],
        out_specs=(pl.BlockSpec(memory_space=pltpu.VMEM), pl.BlockSpec(memory_space=pltpu.VMEM)),
        scratch_shapes=[
            pltpu.VMEM(x.shape, x.dtype),
            pltpu.VMEM(x.shape, x.dtype),
            pltpu.VMEM((steps + 1, width, width), x.dtype),
            pltpu.VMEM((steps, width, width), x.dtype),
            pltpu.SemaphoreType.DMA((slots,)),
            pltpu.SemaphoreType.DMA((slots,)),
        ],
        compiler_params=pltpu.CompilerParams(collective_id=3, has_side_effects=True),
    )(x)


def local(error, covar, basis):
    dot = functools.partial(lax.dot_general, precision=lax.Precision.HIGH, preferred_element_type=jnp.float32)
    across = (((0,), (0,)), ((), ()))
    along = (((1,), (0,)), ((), ()))
    current = basis
    lower = None
    for step in range(ITERS):
        projected = sum_rows(dot(error, current, across))
        needed = turn(dot(covar, projected, along))
        block, gram = block_gram(dot(error, needed, along))
        lower = jnp.linalg.cholesky(gram)
        current = lax.linalg.triangular_solve(
            lower, block, left_side=False, lower=True, transpose_a=True
        )
    return (current, lower.T)


def solution(mesh):
    in_specs = (P("row", "col"), P("row", "col"), P("row", None))
    out_specs = (P("row", None), P())
    return jax.shard_map(local, mesh=mesh, in_specs=in_specs, out_specs=out_specs, check_vma=False)
```
